768 devices in a mesh: space: 192 (over z_hi, y, x, core), orb: 4 (over z_lo).
Axes of the slice: x: 4, y: 8, z: 12 (z_hi: 3, z_lo: 4; z = z_hi * 4 + z_lo), core: 2. Of those that a mesh axis runs over, the one named last changes fastest.
Arguments:
- wavefunctions: float32 [192, 1536, 384], P('space', None, 'orb'), may hold values from -70 to 70
- cell_ham: float32 [192, 4, 729, 729], P('space'), may hold values from -1 to 1, as said below
- cell_nodes: int32 [192, 4, 729], P('space'), may hold values from 0 to 1535, as said below
- cell_count: int32 [192], P('space'), may hold values from 2 to 4, as said below
- upper_nodes: int32 [192, 512], P('space'), may hold values from 0 to 1536, as said below
- lower_nodes: int32 [192, 512], P('space'), may hold values from 0 to 1536, as said below
Outputs:
- rotated: float32 [192, 1536, 384], P('space', 'orb')
The draws below stay inside these ranges and needn't reach their ends.
Inputs may be any that keep to these rules, and one draw needn't show every extreme that they name: `cell_nodes`: each cell's 729 entries are distinct. `cell_count`: some part has 4 live cells. Entries equal to 1536 are empty slots and come after the live ones; for p < 191, upper_nodes[p, k] is live exactly where lower_nodes[p + 1, k] is, and the two name the same shared node; the live entries of upper_nodes[p] and lower_nodes[p] are all distinct; the last part's list is empty; some list has all 512 slots live. `lower_nodes`: paired with upper_nodes as stated there; the first part's list is empty. `cell_ham`: each cell's matrix is symmetric.
All inputs are finite; a program needn't handle non-finite values.
Results may differ from the reference program's by a relative error of at most 0.0003.
Values sent between devices are 32-bit elements; how exact they have to be, the bound alone decides.
No kernel may reach another device: no remote copies, remote signals or barrier semaphores. Data moves between devices by JAX's collectives and lax.ppermute only.
A program may use at most 64 MiB of HBM per device.

```python
import math
import jax
import jax.numpy as jnp
from jax import lax

COLS = 384
CELL_NODES = 729
CAP = 4
NODES_DEV = 1536
DEGREE = 3
SHARE = 512
N_SPACE = 192


def draw_wavefunctions(key, part):
    key_base, key_node, key_column = jax.random.split(key, 3)
    device_rank = jnp.arange(N_SPACE, dtype=jnp.float32)
    amplitude = jnp.sqrt(1.0 + 2.0 * device_rank / max(N_SPACE - 1, 1))[:, None, None]
    node_scale = jnp.exp(jax.random.uniform(key_node, (N_SPACE, NODES_DEV, 1), jnp.float32, math.log(0.5), math.log(5.0)))
    column_scale = jnp.exp(jax.random.uniform(key_column, (1, 1, COLS), jnp.float32, math.log(0.5), math.log(2.0)))
    entries = jnp.clip(jax.random.normal(key_base, (N_SPACE, NODES_DEV, COLS), jnp.float32), -4.0, 4.0)
    return entries * amplitude * node_scale * column_scale


def draw_cell_ham(key, part):
    subkeys = jax.random.split(key, N_SPACE)

    def one_device(device_key):
        entries = jnp.clip(jax.random.normal(device_key, (CAP, CELL_NODES, CELL_NODES), jnp.float32), -4.0, 4.0)
        return (entries + jnp.swapaxes(entries, 1, 2)) * (0.5 / math.sqrt(2.0 * CELL_NODES))
    return lax.map(one_device, subkeys)


def draw_cell_nodes(key, part):
    subkeys = jax.random.split(key, N_SPACE * CAP)
    orderings = jax.vmap(lambda cell_key: jax.random.permutation(cell_key, NODES_DEV)[:CELL_NODES])(subkeys)
    return orderings.reshape(N_SPACE, CAP, CELL_NODES).astype(jnp.int32)


def draw_cell_count(key, part):
    key_count, key_chosen = jax.random.split(key, 2)
    counts = jax.random.randint(key_count, (N_SPACE,), CAP // 2, CAP + 1, jnp.int32)
    chosen = jax.random.randint(key_chosen, (), 0, N_SPACE, jnp.int32)
    return counts.at[chosen].set(CAP).astype(jnp.int32)


def shared_lists(key):
    base_key = jax.random.fold_in(key, 11)
    key_order, key_length, key_chosen = jax.random.split(base_key, 3)
    orderings = jax.vmap(lambda device_key: jax.random.permutation(device_key, NODES_DEV))(jax.random.split(key_order, N_SPACE)).astype(jnp.int32)
    lengths = jax.random.randint(key_length, (N_SPACE,), SHARE // 2, SHARE + 1, jnp.int32)
    chosen = jax.random.randint(key_chosen, (), 0, N_SPACE - 1, jnp.int32)
    lengths = lengths.at[chosen].set(SHARE).at[N_SPACE - 1].set(0)
    lengths_below = jnp.concatenate([jnp.zeros((1,), jnp.int32), lengths[:-1]])
    slot_rank = jnp.arange(SHARE, dtype=jnp.int32)
    upper_lists = jnp.where(slot_rank[None, :] < lengths[:, None], orderings[:, :SHARE], NODES_DEV)
    lower_lists = jnp.where(slot_rank[None, :] < lengths_below[:, None], orderings[:, SHARE:2 * SHARE], NODES_DEV)
    return (upper_lists.astype(jnp.int32), lower_lists.astype(jnp.int32))


def draw_upper_nodes(key, part):
    return shared_lists(key)[0]


def draw_lower_nodes(key, part):
    return shared_lists(key)[1]


def setup_inputs(seed: int = 0) -> dict:
    keys = jax.random.split(jax.random.key(seed), 7)
    wavefunctions = draw_wavefunctions(jax.random.fold_in(keys[6], 71), 0)
    cell_ham = draw_cell_ham(jax.random.fold_in(keys[6], 71), 0)
    cell_nodes = draw_cell_nodes(jax.random.fold_in(keys[6], 71), 0)
    cell_count = draw_cell_count(jax.random.fold_in(keys[6], 71), 0)
    upper_nodes = draw_upper_nodes(jax.random.fold_in(keys[6], 71), 0)
    lower_nodes = draw_lower_nodes(jax.random.fold_in(keys[6], 71), 0)
    return {"wavefunctions": wavefunctions, "cell_ham": cell_ham, "cell_nodes": cell_nodes, "cell_count": cell_count, "upper_nodes": upper_nodes, "lower_nodes": lower_nodes}


center_shift = 0.5
half_width = 2.0

def assemble_all(nodal_field, cell_ham, cell_nodes, cell_count):

    def per_device(device_args):
        values, matrices, node_map, live_cells = device_args
        assembled = jnp.zeros_like(values)
        for cell_slot in range(CAP):
            rows = node_map[cell_slot]
            product = lax.dot_general(matrices[cell_slot].astype(jnp.float32), jnp.take(values, rows, axis=0).astype(jnp.float32), (((0,), (0,)), ((), ())), precision=lax.Precision.HIGHEST, preferred_element_type=jnp.float32)
            keep_cell = (cell_slot < live_cells).astype(jnp.float32)
            assembled = assembled.at[rows].add(product * keep_cell)
        return assembled
    return lax.map(per_device, (nodal_field, cell_ham, cell_nodes, cell_count))

def fetch_rims(values, positions):
    return values.at[positions].get(mode='fill', fill_value=0.0)

def place_rims(values, upper_list, lower_list, from_above, from_below):
    return values.at[upper_list].add(from_above, mode='drop').at[lower_list].add(from_below, mode='drop')

def operate(nodal_field, cell_ham, cell_nodes, cell_count, upper_nodes, lower_nodes):
    assembled = assemble_all(nodal_field, cell_ham, cell_nodes, cell_count)
    upper_values = jax.vmap(fetch_rims)(assembled, upper_nodes)
    lower_values = jax.vmap(fetch_rims)(assembled, lower_nodes)
    no_values = jnp.zeros_like(upper_values[:1])
    from_above = jnp.concatenate([lower_values[1:], no_values], axis=0)
    from_below = jnp.concatenate([no_values, upper_values[:-1]], axis=0)
    return jax.vmap(place_rims)(assembled, upper_nodes, lower_nodes, from_above, from_below)

def reference(wavefunctions, cell_ham, cell_nodes, cell_count, upper_nodes, lower_nodes):
    start_field = wavefunctions
    previous = start_field
    current = (operate(start_field, cell_ham, cell_nodes, cell_count, upper_nodes, lower_nodes) - center_shift * start_field) / half_width
    for repeat in range(DEGREE - 1):
        following = 2.0 * (operate(current, cell_ham, cell_nodes, cell_count, upper_nodes, lower_nodes) - center_shift * current) / half_width - previous
        previous, current = (current, following)
    weight = jax.vmap(lambda lower_list: jnp.ones((NODES_DEV,), jnp.float32).at[lower_list].set(0.0, mode='drop'))(lower_nodes)
    weight = weight * (1.0 / (N_SPACE * NODES_DEV))
    gram_total = jnp.einsum('pnc,pnd->cd', current * weight[:, :, None], current, precision=lax.Precision.HIGHEST)
    factor = jnp.linalg.cholesky(gram_total)
    filtered = current.reshape(N_SPACE * NODES_DEV, COLS)
    solved = lax.linalg.triangular_solve(factor, filtered, left_side=False, lower=True, transpose_a=True)
    return solved.reshape(N_SPACE, NODES_DEV, COLS)
```

```python
import functools

import jax
import jax.numpy as jnp
from jax import lax
from jax.experimental import pallas as pl
from jax.experimental.pallas import tpu as pltpu
from jax.sharding import Mesh, PartitionSpec as P

DEGREE = 3
CAP = 4
CELL = 729
NODES = 1536
ROWS = 1544
COLS = 384
OWN = 96
SHARE = 512
BLK = 128

center_shift = 0.5
half_width = 2.0

SPACE = ("z_hi", "y", "x", "core")
NEAR = ("x", "core", "orb")
FAR = ("z_hi", "y")

F32 = jnp.float32
BF16 = jnp.bfloat16
NT = (((1,), (1,)), ((), ()))
NN = (((1,), (0,)), ((), ()))
TN = (((0,), (0,)), ((), ()))
VMEM_BYTES = 56 * 1024 * 1024


def halves(value):
    high = value.astype(BF16)
    low = (value - high.astype(F32)).astype(BF16)
    return high, low


def dot(a, b, dims):
    return lax.dot_general(a, b, dims, preferred_element_type=F32)


def dot_exact(a, b, dims):
    return lax.dot_general(a, b, dims, precision=lax.Precision.HIGHEST, preferred_element_type=F32)


def dot_three(a, b, dims):
    a_high, a_low = halves(a)
    b_high, b_low = halves(b)
    return dot(a_high, b_high, dims) + (dot(a_high, b_low, dims) + dot(a_low, b_high, dims))


def add_rims(field, list_ref, arrived, scale):
    step = 16

    def some(i, carry):
        first = i * step
        picks = [list_ref[first + j] for j in range(step)]
        new = [field[pl.ds(picks[j], 1), :] + arrived[pl.ds(first + j, 1), :] * scale for j in range(step)]
        for j in range(step):
            field[pl.ds(picks[j], 1), :] = new[j]
        return carry

    lax.fori_loop(0, SHARE // step, some, 0)


def take_rims(field, list_ref, out):
    step = 16

    def some(i, carry):
        first = i * step
        rows = [field[pl.ds(list_ref[first + j], 1), :] for j in range(step)]
        for j in range(step):
            out[pl.ds(first + j, 1), :] = rows[j]
        return carry

    lax.fori_loop(0, SHARE // step, some, 0)


def take_cell(field, nodes_ref, cell, out):
    step = 27

    def some(i, carry):
        first = i * step
        rows = [field[pl.ds(nodes_ref[cell * CELL + first + j], 1), :] for j in range(step)]
        for j in range(step):
            out[pl.ds(first + j, 1), :] = rows[j]
        return carry

    lax.fori_loop(0, CELL // step, some, 0)


def add_cell(total, nodes_ref, cell, product):
    step = 27

    def some(i, carry):
        first = i * step
        picks = [nodes_ref[cell * CELL + first + j] for j in range(step)]
        new = [total[pl.ds(picks[j], 1), :] + product[pl.ds(first + j, 1), :] for j in range(step)]
        for j in range(step):
            total[pl.ds(picks[j], 1), :] = new[j]
        return carry

    lax.fori_loop(0, CELL // step, some, 0)


def cell_work(cell, nodes_ref, high, low, field, total, gathered, packed, product):
    take_cell(field, nodes_ref, cell, gathered)
    rows = gathered[0:CELL, :]
    rows_high, rows_low = halves(rows)
    packed[:, 0:BLK] = rows_high
    packed[:, BLK:] = rows_low
    both = dot(high[...], packed[...], NN)
    rest = dot(low[...], packed[:, 0:BLK], NN)
    product[0:CELL, :] = both[:, 0:BLK] + (both[:, BLK:] + rest)
    add_cell(total, nodes_ref, cell, product)


def finish_step(field, total, previous, scale, upper_ref, lower_ref, next_out, up_out, low_out):
    step = total[0:NODES, :] - center_shift * field[0:NODES, :]
    step = step * scale
    if previous is not None:
        step = step - previous
    next_out[...] = step
    take_rims(total, upper_ref, up_out)
    take_rims(total, lower_ref, low_out)


def first_kernel(live_ref, nodes_ref, upper_ref, lower_ref, start_ref, ham_ref, next_out, up_out, low_out, high_out, low_part_out, field, total, gathered, packed, product):
    cell = pl.program_id(0)

    @pl.when(cell == 0)
    def _():
        field[...] = jnp.zeros_like(field)
        field[0:NODES, 0:OWN] = start_ref[0]
        total[...] = jnp.zeros_like(total)

    @pl.when(cell < live_ref[0])
    def _():
        high, low = halves(ham_ref[0, 0])
        high_out[0] = high
        low_part_out[0] = low
        cell_work(cell, nodes_ref, high_out.at[0], low_part_out.at[0], field, total, gathered, packed, product)

    @pl.when(cell == CAP - 1)
    def _():
        finish_step(field, total, None, 1.0 / half_width, upper_ref, lower_ref, next_out, up_out, low_out)


def next_kernel(first, live_ref, nodes_ref, upper_ref, lower_ref, part_ref, prev_ref, from_above_ref, from_below_ref, high_ref, low_ref, field_out, next_out, up_out, low_out, total, gathered, packed, product):
    cell = pl.program_id(0)

    @pl.when(cell == 0)
    def _():
        scale = 1.0 / half_width if first else 1.0
        field_out[0:NODES, :] = part_ref[...]
        field_out[NODES:, :] = jnp.zeros((ROWS - NODES, BLK), F32)
        add_rims(field_out, upper_ref, from_above_ref, scale)
        add_rims(field_out, lower_ref, from_below_ref, scale)
        field_out[NODES:, :] = jnp.zeros((ROWS - NODES, BLK), F32)
        total[...] = jnp.zeros_like(total)

    @pl.when(cell < live_ref[0])
    def _():
        cell_work(cell, nodes_ref, high_ref.at[0], low_ref.at[0], field_out, total, gathered, packed, product)

    @pl.when(cell == CAP - 1)
    def _():
        if first:
            previous = jnp.concatenate([prev_ref[0], jnp.zeros((NODES, BLK - OWN), F32)], axis=1)
        else:
            previous = prev_ref[0:NODES, :]
        finish_step(field_out, total, previous, 1.0, upper_ref, lower_ref, next_out, up_out, low_out)


def last_kernel(upper_ref, lower_ref, part_ref, from_above_ref, from_below_ref, out, weight_out, field, weight):
    field[0:NODES, :] = part_ref[...]
    field[NODES:, :] = jnp.zeros((ROWS - NODES, BLK), F32)
    add_rims(field, upper_ref, from_above_ref, 1.0)
    add_rims(field, lower_ref, from_below_ref, 1.0)
    out[...] = field[0:NODES, 0:OWN]
    weight[...] = jnp.full((ROWS, BLK), 1.0 / (192 * NODES), F32)
    nothing = jnp.zeros((1, BLK), F32)

    def some(i, carry):
        for j in range(16):
            weight[pl.ds(lower_ref[i * 16 + j], 1), :] = nothing
        return carry

    lax.fori_loop(0, SHARE // 16, some, 0)
    weight_out[...] = weight[0:NODES, :]


def gram_kernel(quarter_ref, own_ref, weight_ref, rows_out, gram_out):
    del quarter_ref
    rows = jnp.concatenate([own_ref[0], own_ref[1], own_ref[2], own_ref[3]], axis=1)
    rows_out[...] = rows
    w = weight_ref[...]
    left = jnp.concatenate([rows[:, 0:128] * w, rows[:, 128:256] * w, rows[:, 256:384] * w], axis=1).T
    left_high, left_low = halves(left)
    right_high, right_low = halves(rows)

    def block_row(k):
        a_high, a_low = left_high[k * BLK:(k + 1) * BLK], left_low[k * BLK:(k + 1) * BLK]
        b_high, b_low = right_high[:, :(k + 1) * BLK], right_low[:, :(k + 1) * BLK]
        return dot(a_high, b_high, NN) + (dot(a_high, b_low, NN) + dot(a_low, b_high, NN))

    first, second, third = block_row(0), block_row(1), block_row(2)
    blocks = [first, second[:, :BLK], third[:, :BLK], second[:, BLK:], third[:, BLK:2 * BLK], third[:, 2 * BLK:]]
    for k, block in enumerate(blocks):
        gram_out[k * BLK:(k + 1) * BLK, :] = block


def inverse_factor(work, inverse):
    lane = lax.broadcasted_iota(jnp.int32, (8, BLK), 0)

    def panel(p, carry):
        first = pl.multiple_of(p * 8, 8)
        panel_a = work[pl.ds(first, 8), 0:BLK]
        panel_i = work[pl.ds(first, 8), BLK:]
        turned = pltpu.roll(panel_a, jnp.where(p == 0, 0, BLK - first), 1)
        columns = [jnp.broadcast_to(turned[:, k:k + 1], (8, BLK)) for k in range(8)]
        e = {(i, k): jnp.broadcast_to(columns[k][i:i + 1, :], (8, BLK)) for i in range(8) for k in range(i + 1)}
        rows_a = [jnp.broadcast_to(panel_a[i:i + 1, :], (8, BLK)) for i in range(8)]
        rows_i = [jnp.broadcast_to(panel_i[i:i + 1, :], (8, BLK)) for i in range(8)]
        for k in range(8):
            pivot = e[k, k]
            r = lax.rsqrt(pivot)
            r = r * (1.5 - 0.5 * pivot * r * r)
            rows_a[k] = rows_a[k] * r
            rows_i[k] = rows_i[k] * r
            below = {i: e[i, k] * r for i in range(k + 1, 8)}
            for i in range(k + 1, 8):
                for j in range(k + 1, i + 1):
                    e[i, j] = e[i, j] - below[i] * below[j]
                rows_a[i] = rows_a[i] - below[i] * rows_a[k]
                rows_i[i] = rows_i[i] - below[i] * rows_i[k]
        new_a, new_i = rows_a[0], rows_i[0]
        for k in range(1, 8):
            new_a = jnp.where(lane == k, rows_a[k], new_a)
            new_i = jnp.where(lane == k, rows_i[k], new_i)
        inverse[pl.ds(first, 8), :] = new_i
        both = jnp.concatenate([new_a, new_i], axis=1)

        def three(v):
            v1 = v.astype(BF16).astype(F32)
            rest = v - v1
            v2 = rest.astype(BF16).astype(F32)
            return v1, v2, rest - v2

        a1, a2, a3 = three(new_a)
        b1, b2, b3 = three(both)
        left = jnp.concatenate([a1, a1, a2, a1, a2, a3], axis=0).astype(BF16)
        right = jnp.concatenate([b1, b2, b1, b3, b2, b1], axis=0).astype(BF16)
        work[...] = work[...] - dot(left, right, TN)
        return carry

    lax.fori_loop(0, BLK // 8, panel, 0)


def rotate_kernel(gram_ref, rows_ref, out, work, inverse):
    eye = (lax.broadcasted_iota(jnp.int32, (BLK, BLK), 0) == lax.broadcasted_iota(jnp.int32, (BLK, BLK), 1)).astype(F32)

    def factor(block):
        work[:, 0:BLK] = block
        work[:, BLK:] = eye
        inverse_factor(work, inverse)
        return inverse[...]

    m1 = factor(gram_ref[0:BLK, :])
    left = dot_exact(gram_ref[BLK:3 * BLK, :], m1, NT)
    l21, l31 = left[0:BLK], left[BLK:]
    rows = rows_ref[...]
    z1 = dot_three(rows[:, 0:BLK], m1, NT)
    out[0, :, 0:BLK] = z1
    m2 = factor(gram_ref[3 * BLK:4 * BLK, :] - dot_exact(l21, l21, NT))
    l32 = dot_exact(gram_ref[4 * BLK:5 * BLK, :] - dot_exact(l31, l21, NT), m2, NT)
    z2 = dot_three(rows[:, BLK:2 * BLK] - dot_three(z1, l21, NT), m2, NT)
    out[0, :, BLK:2 * BLK] = z2
    m3 = factor(gram_ref[5 * BLK:, :] - dot_exact(l31, l31, NT) - dot_exact(l32, l32, NT))
    z3 = dot_three(rows[:, 2 * BLK:] - dot_three(z1, l31, NT) - dot_three(z2, l32, NT), m3, NT)
    out[0, :, 2 * BLK:] = z3


def smem():
    return pl.BlockSpec(memory_space=pltpu.SMEM)


def whole(*shape):
    return pl.BlockSpec(shape, lambda *_: (0,) * len(shape))


def params():
    return pltpu.CompilerParams(vmem_limit_bytes=VMEM_BYTES)


def scratch(with_field):
    field = [pltpu.VMEM((ROWS, BLK), F32)] if with_field else []
    return field + [
        pltpu.VMEM((ROWS, BLK), F32),
        pltpu.VMEM((736, BLK), F32),
        pltpu.VMEM((CELL, 2 * BLK), BF16),
        pltpu.VMEM((736, BLK), F32),
    ]


def struct(*shape, dtype=F32):
    return jax.ShapeDtypeStruct(shape, dtype)


def first_step(live, nodes, upper, lower, start, ham):
    cell_block = pl.BlockSpec((1, CELL, CELL), lambda c: (c, 0, 0))
    return pl.pallas_call(
        first_kernel,
        grid=(CAP,),
        in_specs=[smem(), smem(), smem(), smem(), whole(1, NODES, OWN), pl.BlockSpec((1, 1, CELL, CELL), lambda c: (0, c, 0, 0))],
        out_specs=[whole(NODES, BLK), whole(SHARE, BLK), whole(SHARE, BLK), cell_block, cell_block],
        out_shape=[struct(NODES, BLK), struct(SHARE, BLK), struct(SHARE, BLK), struct(CAP, CELL, CELL, dtype=BF16), struct(CAP, CELL, CELL, dtype=BF16)],
        scratch_shapes=scratch(True),
        compiler_params=params(),
        name="first_step",
    )(live, nodes, upper, lower, start, ham)


def next_step(first, live, nodes, upper, lower, part, previous, above, below, high, low):
    cell_block = pl.BlockSpec((1, CELL, CELL), lambda c: (c, 0, 0))
    return pl.pallas_call(
        functools.partial(next_kernel, first),
        grid=(CAP,),
        in_specs=[smem(), smem(), smem(), smem(), whole(NODES, BLK), whole(*previous.shape), whole(SHARE, BLK), whole(SHARE, BLK), cell_block, cell_block],
        out_specs=[whole(ROWS, BLK), whole(NODES, BLK), whole(SHARE, BLK), whole(SHARE, BLK)],
        out_shape=[struct(ROWS, BLK), struct(NODES, BLK), struct(SHARE, BLK), struct(SHARE, BLK)],
        scratch_shapes=scratch(False),
        compiler_params=params(),
        name="second_step" if first else "third_step",
    )(live, nodes, upper, lower, part, previous, above, below, high, low)


def last_step(upper, lower, part, above, below):
    return pl.pallas_call(
        last_kernel,
        in_specs=[smem(), smem()] + [pl.BlockSpec(memory_space=pltpu.VMEM)] * 3,
        out_specs=[pl.BlockSpec(memory_space=pltpu.VMEM)] * 2,
        out_shape=[struct(NODES, OWN), struct(NODES, BLK)],
        scratch_shapes=[pltpu.VMEM((ROWS, BLK), F32)] * 2,
        compiler_params=params(),
        name="last_step",
    )(upper, lower, part, above, below)


def gram_step(quarter, own, weight):
    return pl.pallas_call(
        gram_kernel,
        grid_spec=pltpu.PrefetchScalarGridSpec(
            num_scalar_prefetch=1,
            grid=(1,),
            in_specs=[whole(4, COLS, OWN), pl.BlockSpec((COLS, BLK), lambda i, q: (q[0], 0))],
            out_specs=[whole(COLS, COLS), whole(6 * BLK, BLK)],
        ),
        out_shape=[struct(COLS, COLS), struct(6 * BLK, BLK)],
        compiler_params=params(),
        name="gram_step",
    )(quarter, own, weight)


def rotate_step(gram, rows):
    return pl.pallas_call(
        rotate_kernel,
        out_shape=struct(1, COLS, COLS),
        scratch_shapes=[pltpu.VMEM((BLK, 2 * BLK), F32), pltpu.VMEM((BLK, BLK), F32)],
        compiler_params=params(),
        name="rotate_step",
    )(gram, rows)


def exchange(up, low):
    last = 191
    from_above = lax.ppermute(low, SPACE, [(i + 1, i) for i in range(last)])
    from_below = lax.ppermute(up, SPACE, [(i, i + 1) for i in range(last)])
    return from_above, from_below


def scatter_sum(value, axes):
    parts = lax.axis_size(axes)
    pieces = lax.all_to_all(value.reshape(parts, -1, BLK), axes, 0, 0, tiled=True)
    return pieces.sum(0)


def total_sum(value, axes):
    parts = lax.axis_size(axes)
    copies = jnp.broadcast_to(value[None], (parts,) + value.shape)
    return lax.all_to_all(copies, axes, 0, 0, tiled=True).sum(0)


def spread(value, axes):
    parts = lax.axis_size(axes)
    copies = jnp.broadcast_to(value[None], (parts,) + value.shape)
    return lax.all_to_all(copies, axes, 0, 0, tiled=True).reshape(-1, BLK)


def shards(wavefunctions, cell_ham, cell_nodes, cell_count, upper_nodes, lower_nodes):
    nodes = cell_nodes.reshape(-1)
    upper = upper_nodes.reshape(-1)
    lower = lower_nodes.reshape(-1)
    part, up, low, ham_high, ham_low = first_step(cell_count, nodes, upper, lower, wavefunctions, cell_ham)
    above, below = exchange(up, low)
    previous = wavefunctions
    for repeat in range(DEGREE - 1):
        current, part, up, low = next_step(repeat == 0, cell_count, nodes, upper, lower, part, previous, above, below, ham_high, ham_low)
        above, below = exchange(up, low)
        previous = current
    filtered, weight = last_step(upper, lower, part, above, below)
    own = lax.all_to_all(filtered.reshape(4, COLS, OWN), "orb", 0, 0, tiled=True)
    quarter = lax.axis_index("orb").astype(jnp.int32).reshape(1)
    rows, gram = gram_step(quarter, own, weight)
    gram = spread(total_sum(scatter_sum(gram, NEAR), FAR), NEAR)
    return rotate_step(gram, rows)


def solution(mesh):
    fine = Mesh(mesh.devices.reshape(3, 8, 4, 2, 4), SPACE + ("orb",))
    in_specs = (
        P(SPACE, None, "orb"),
        P(SPACE, None, None, None),
        P(SPACE, None, None),
        P(SPACE),
        P(SPACE, None),
        P(SPACE, None),
    )
    out_specs = P(SPACE, "orb", None)
    return jax.shard_map(shards, mesh=fine, in_specs=in_specs, out_specs=out_specs, check_vma=False)
```

```python
import functools

import jax
import jax.numpy as jnp
from jax import lax
from jax.experimental import pallas as pl
from jax.experimental.pallas import tpu as pltpu
from jax.sharding import Mesh, PartitionSpec as P

DEGREE = 3
CAP = 4
CELL = 729
NODES = 1536
ROWS = 1544
COLS = 384
OWN = 96
SHARE = 512
BLK = 128

center_shift = 0.5
half_width = 2.0

SPACE = ("z_hi", "y", "x", "core")
NEAR = ("x", "core", "orb")
FAR = ("z_hi", "y")

F32 = jnp.float32
BF16 = jnp.bfloat16
NT = (((1,), (1,)), ((), ()))
NN = (((1,), (0,)), ((), ()))
TN = (((0,), (0,)), ((), ()))
VMEM_BYTES = 56 * 1024 * 1024


def halves(value):
    high = value.astype(BF16)
    low = (value - high.astype(F32)).astype(BF16)
    return high, low


def dot(a, b, dims):
    return lax.dot_general(a, b, dims, preferred_element_type=F32)


def dot_exact(a, b, dims):
    return lax.dot_general(a, b, dims, precision=lax.Precision.HIGHEST, preferred_element_type=F32)


def dot_three(a, b, dims):
    a_high, a_low = halves(a)
    b_high, b_low = halves(b)
    return dot(a_high, b_high, dims) + (dot(a_high, b_low, dims) + dot(a_low, b_high, dims))


def add_rims(field, upper_ref, lower_ref, above, below, scale):
    step = 16

    def some(i, carry):
        first = i * step
        picks = [upper_ref[first + j] for j in range(step)] + [lower_ref[first + j] for j in range(step)]
        new = [field[pl.ds(picks[j], 1), :] + above[pl.ds(first + j, 1), :] * scale for j in range(step)]
        new += [field[pl.ds(picks[step + j], 1), :] + below[pl.ds(first + j, 1), :] * scale for j in range(step)]
        for j in range(2 * step):
            field[pl.ds(picks[j], 1), :] = new[j]
        return carry

    lax.fori_loop(0, SHARE // step, some, 0)


def take_rims(field, upper_ref, lower_ref, up, low):
    step = 16

    def some(i, carry):
        first = i * step
        up_rows = [field[pl.ds(upper_ref[first + j], 1), :] for j in range(step)]
        low_rows = [field[pl.ds(lower_ref[first + j], 1), :] for j in range(step)]
        for j in range(step):
            up[pl.ds(first + j, 1), :] = up_rows[j]
            low[pl.ds(first + j, 1), :] = low_rows[j]
        return carry

    lax.fori_loop(0, SHARE // step, some, 0)


def pack_rims(rim, out):
    lane = lax.broadcasted_iota(jnp.int32, (BLK, BLK), 1)
    tail = rim[3 * BLK:, :]
    for j in range(3):
        moved = pltpu.roll(tail, OWN - 32 * j, 1)
        out[j * BLK:(j + 1) * BLK, :] = jnp.where(lane < OWN, rim[j * BLK:(j + 1) * BLK, :], moved)


def unpack_rims(packed, rim):
    lane = lax.broadcasted_iota(jnp.int32, (BLK, BLK), 1)
    rim[0:3 * BLK, :] = packed[...]
    tail = pltpu.roll(packed[0:BLK, :], 32, 1)
    tail = jnp.where(lane < 32, tail, pltpu.roll(packed[BLK:2 * BLK, :], 64, 1))
    rim[3 * BLK:, :] = jnp.where(lane < 64, tail, pltpu.roll(packed[2 * BLK:, :], 96, 1))


def take_cell(field, nodes_ref, cell, out):
    step = 27
    base = cell * CELL

    def some(i, carry):
        first = i * step
        rows = [field[pl.ds(nodes_ref[base + first + j], 1), :] for j in range(step)]
        for j in range(step):
            out[pl.ds(first + j, 1), :] = rows[j]
        return carry

    lax.fori_loop(0, CELL // step, some, 0)


def put_cell(parts, nodes_ref, cell, product):
    step = 27
    base = cell * CELL
    first_row = cell * ROWS

    def some(i, carry):
        first = i * step
        rows = [product[pl.ds(first + j, 1), :] for j in range(step)]
        for j in range(step):
            parts[pl.ds(first_row + nodes_ref[base + first + j], 1), :] = rows[j]
        return carry

    lax.fori_loop(0, CELL // step, some, 0)


def multiply_cell(high, low, gathered, packed, product):
    rows_high, rows_low = halves(gathered[0:CELL, :])
    packed[:, 0:BLK] = rows_high
    packed[:, BLK:] = rows_low
    both = dot(high[...], packed[...], NN)
    rest = dot(low[...], packed[:, 0:BLK], NN)
    product[0:CELL, :] = both[:, 0:BLK] + (both[:, BLK:] + rest)


def finish_step(field, parts, total, rims, previous, scale, upper_ref, lower_ref, next_out, up_out, low_out):
    total[...] = (parts[0:ROWS] + parts[ROWS:2 * ROWS]) + (parts[2 * ROWS:3 * ROWS] + parts[3 * ROWS:])
    take_rims(total, upper_ref, lower_ref, rims.at[0], rims.at[1])
    pack_rims(rims.at[0], up_out)
    pack_rims(rims.at[1], low_out)
    step = total[0:NODES, :] - center_shift * field[0:NODES, :]
    step = step * scale
    if previous is not None:
        step = step - previous[...]
    next_out[...] = step


def first_kernel(live_ref, nodes_ref, upper_ref, lower_ref, start_ref, ham_ref, next_out, up_out, low_out, high_out, low_part_out, field_out, field, parts, total, rims, gathered, packed, product, ham, sems):
    cell = pl.program_id(0)
    fetches = [pltpu.make_async_copy(ham_ref.at[:, slot, :], ham.at[slot], sems.at[slot]) for slot in range(CAP)]
    save = pltpu.make_async_copy(field.at[0:NODES, :], field_out, sems.at[CAP])

    @pl.when(cell == 0)
    def _():
        for fetch in fetches:
            fetch.start()
        field[0:NODES, :] = jnp.concatenate([start_ref[0], jnp.zeros((BLK - OWN, NODES), F32)], axis=0).T
        field[NODES:, :] = jnp.zeros((ROWS - NODES, BLK), F32)
        save.start()
        parts[...] = jnp.zeros_like(parts)

    @pl.when(cell < live_ref[0])
    def _():
        take_cell(field, nodes_ref, cell, gathered)

    for slot in range(CAP):
        @pl.when(cell == slot)
        def _():
            fetches[slot].wait()

    @pl.when(cell < live_ref[0])
    def _():
        high, low = halves(ham[cell])
        high_out[0] = high
        low_part_out[0] = low

    @pl.when(cell < live_ref[0])
    def _():
        multiply_cell(high_out.at[0], low_part_out.at[0], gathered, packed, product)
        put_cell(parts, nodes_ref, cell, product)

    @pl.when(cell == CAP - 1)
    def _():
        finish_step(field, parts, total, rims, None, 1.0 / half_width, upper_ref, lower_ref, next_out, up_out, low_out)
        save.wait()


def next_kernel(first, live_ref, nodes_ref, upper_ref, lower_ref, part_ref, prev_ref, above_ref, below_ref, high_ref, low_ref, *rest):
    if first:
        next_out, up_out, low_out, field_out, field, parts, total, rims, gathered, packed, product, previous, arrived, sems = rest
    else:
        next_out, up_out, low_out, field, parts, total, rims, gathered, packed, product, previous, arrived, sems = rest
    cell = pl.program_id(0)
    fetch = pltpu.make_async_copy(prev_ref, previous, sems.at[0])
    from_above = pltpu.make_async_copy(above_ref, arrived.at[0], sems.at[1])
    from_below = pltpu.make_async_copy(below_ref, arrived.at[1], sems.at[2])

    @pl.when(cell == 0)
    def _():
        from_above.start()
        from_below.start()
        fetch.start()
        scale = 1.0 / half_width if first else 1.0
        field[0:NODES, :] = part_ref[...]
        field[NODES:, :] = jnp.zeros((ROWS - NODES, BLK), F32)
        parts[...] = jnp.zeros_like(parts)
        from_above.wait()
        unpack_rims(arrived.at[0], rims.at[0])
        from_below.wait()
        unpack_rims(arrived.at[1], rims.at[1])
        add_rims(field, upper_ref, lower_ref, rims.at[0], rims.at[1], scale)
        field[NODES:, :] = jnp.zeros((ROWS - NODES, BLK), F32)
        if first:
            pltpu.make_async_copy(field.at[0:NODES, :], field_out, sems.at[3]).start()

    @pl.when(cell < live_ref[0])
    def _():
        take_cell(field, nodes_ref, cell, gathered)
        multiply_cell(high_ref.at[0], low_ref.at[0], gathered, packed, product)
        put_cell(parts, nodes_ref, cell, product)

    @pl.when(cell == CAP - 1)
    def _():
        fetch.wait()
        finish_step(field, parts, total, rims, previous, 1.0, upper_ref, lower_ref, next_out, up_out, low_out)
        if first:
            pltpu.make_async_copy(field.at[0:NODES, :], field_out, sems.at[3]).wait()


def last_kernel(upper_ref, lower_ref, part_ref, above_ref, below_ref, out, field, rims):
    field[0:NODES, :] = part_ref[...]
    field[NODES:, :] = jnp.zeros((ROWS - NODES, BLK), F32)
    unpack_rims(above_ref, rims.at[0])
    unpack_rims(below_ref, rims.at[1])
    add_rims(field, upper_ref, lower_ref, rims.at[0], rims.at[1], 1.0)
    turned = field[0:NODES, :].T[0:OWN, :]
    for q in range(4):
        out[q] = turned[:, q * COLS:(q + 1) * COLS]


def weight_kernel(lower_ref, out, weight):
    weight[...] = jnp.full((ROWS, BLK), 1.0 / (192 * NODES), F32)
    nothing = jnp.zeros((1, BLK), F32)

    def some(i, carry):
        for j in range(16):
            weight[pl.ds(lower_ref[i * 16 + j], 1), :] = nothing
        return carry

    lax.fori_loop(0, SHARE // 16, some, 0)
    out[...] = weight[0:NODES, :].T[0:8, :]


def gram_kernel(quarter_ref, own_ref, weight_ref, rows_out, gram_out):
    del quarter_ref
    turned = own_ref[...]
    rows_out[...] = turned.T
    left_high, left_low = halves(turned * weight_ref[0:1, :])
    right_high, right_low = halves(turned)

    def block_row(k):
        a_high, a_low = left_high[k * BLK:(k + 1) * BLK], left_low[k * BLK:(k + 1) * BLK]
        b_high, b_low = right_high[:(k + 1) * BLK], right_low[:(k + 1) * BLK]
        return dot(a_high, b_high, NT) + (dot(a_high, b_low, NT) + dot(a_low, b_high, NT))

    first, second, third = block_row(0), block_row(1), block_row(2)
    blocks = [first, second[:, :BLK], third[:, :BLK], second[:, BLK:], third[:, BLK:2 * BLK], third[:, 2 * BLK:]]
    for k, block in enumerate(blocks):
        gram_out[k * BLK:(k + 1) * BLK, :] = block


def inverse_factor(work, inverse, left_ref, right_ref):
    sub = lax.broadcasted_iota(jnp.int32, (8, BLK), 0)
    lane = lax.broadcasted_iota(jnp.int32, (8, BLK), 1)
    left_ref[...] = jnp.zeros_like(left_ref)
    right_ref[...] = jnp.zeros_like(right_ref)

    def three(v):
        v1 = v.astype(BF16).astype(F32)
        rest = v - v1
        v2 = rest.astype(BF16).astype(F32)
        return v1, v2, rest - v2

    def panel(p, carry):
        panel_a, panel_i = carry
        first = pl.multiple_of(p * 8, 8)
        work[...] = work[...] - dot(left_ref[...], right_ref[...], TN)
        columns = [jnp.broadcast_to(jnp.sum(jnp.where(lane == first + k, panel_a, 0.0), axis=1, keepdims=True), (8, BLK)) for k in range(8)]
        e = {(i, k): jnp.broadcast_to(columns[k][i:i + 1, :], (8, BLK)) for i in range(8) for k in range(i + 1)}
        rows_a = [jnp.broadcast_to(panel_a[i:i + 1, :], (8, BLK)) for i in range(8)]
        rows_i = [jnp.broadcast_to(panel_i[i:i + 1, :], (8, BLK)) for i in range(8)]
        for k in range(8):
            pivot = e[k, k]
            r = lax.rsqrt(pivot)
            r = r * (1.5 - 0.5 * pivot * r * r)
            rows_a[k] = rows_a[k] * r
            rows_i[k] = rows_i[k] * r
            below = {i: e[i, k] * r for i in range(k + 1, 8)}
            for i in range(k + 1, 8):
                for j in range(k + 1, i + 1):
                    e[i, j] = e[i, j] - below[i] * below[j]
                rows_a[i] = rows_a[i] - below[i] * rows_a[k]
                rows_i[i] = rows_i[i] - below[i] * rows_i[k]
        new_a, new_i = rows_a[0], rows_i[0]
        for k in range(1, 8):
            new_a = jnp.where(sub == k, rows_a[k], new_a)
            new_i = jnp.where(sub == k, rows_i[k], new_i)
        inverse[pl.ds(first, 8), :] = new_i
        a1, a2, a3 = three(new_a)
        b1, b2, b3 = three(jnp.concatenate([new_a, new_i], axis=1))
        left_ref[...] = jnp.concatenate([a1, a1, a2, a1, a2, a3], axis=0).astype(BF16)
        right_ref[...] = jnp.concatenate([b1, b2, b1, b3, b2, b1], axis=0).astype(BF16)
        following = pl.multiple_of(jnp.minimum(first + 8, BLK - 8), 8)
        next_a = work[pl.ds(following, 8), 0:BLK]
        next_i = work[pl.ds(following, 8), BLK:]
        for k in range(8):
            factor = jnp.sum(jnp.where(lane == sub + (first + 8), rows_a[k], 0.0), axis=1, keepdims=True)
            next_a = next_a - factor * rows_a[k]
            next_i = next_i - factor * rows_i[k]
        return next_a, next_i

    lax.fori_loop(0, BLK // 8, panel, (work[0:8, 0:BLK], work[0:8, BLK:]))


def rotate_kernel(gram_ref, rows_ref, out, work, inverse, left_ref, right_ref):
    eye = (lax.broadcasted_iota(jnp.int32, (BLK, BLK), 0) == lax.broadcasted_iota(jnp.int32, (BLK, BLK), 1)).astype(F32)

    def factor(block):
        work[:, 0:BLK] = block
        work[:, BLK:] = eye
        inverse_factor(work, inverse, left_ref, right_ref)
        return inverse[...]

    m1 = factor(gram_ref[0:BLK, :])
    left = dot_exact(gram_ref[BLK:3 * BLK, :], m1, NT)
    l21, l31 = left[0:BLK], left[BLK:]
    m2 = factor(gram_ref[3 * BLK:4 * BLK, :] - dot_exact(l21, l21, NT))
    l32 = dot_exact(gram_ref[4 * BLK:5 * BLK, :] - dot_exact(l31, l21, NT), m2, NT)
    rows = rows_ref[...]
    z1 = dot_three(rows[:, 0:BLK], m1, NT)
    out[0, :, 0:BLK] = z1
    z2 = dot_three(rows[:, BLK:2 * BLK] - dot_three(z1, l21, NT), m2, NT)
    out[0, :, BLK:2 * BLK] = z2
    m3 = factor(gram_ref[5 * BLK:, :] - dot_exact(l31, l31, NT) - dot_exact(l32, l32, NT))
    z3 = dot_three(rows[:, 2 * BLK:] - dot_three(z1, l31, NT) - dot_three(z2, l32, NT), m3, NT)
    out[0, :, 2 * BLK:] = z3


def smem():
    return pl.BlockSpec(memory_space=pltpu.SMEM)


def anywhere():
    return pl.BlockSpec(memory_space=pl.ANY)


def vmem():
    return pl.BlockSpec(memory_space=pltpu.VMEM)


def whole(*shape):
    return pl.BlockSpec(shape, lambda *_: (0,) * len(shape))


def params():
    return pltpu.CompilerParams(vmem_limit_bytes=VMEM_BYTES)


def scratch(*more):
    return [
        pltpu.VMEM((ROWS, BLK), F32),
        pltpu.VMEM((CAP * ROWS, BLK), F32),
        pltpu.VMEM((ROWS, BLK), F32),
        pltpu.VMEM((2, SHARE, BLK), F32),
        pltpu.VMEM((736, BLK), F32),
        pltpu.VMEM((CELL, 2 * BLK), BF16),
        pltpu.VMEM((736, BLK), F32),
        *more,
        pltpu.SemaphoreType.DMA((5,)),
    ]


def struct(*shape, dtype=F32):
    return jax.ShapeDtypeStruct(shape, dtype)


PACKED = 3 * BLK


def first_step(live, nodes, upper, lower, start, ham):
    cell_block = pl.BlockSpec((1, CELL, CELL), lambda c: (c, 0, 0))
    return pl.pallas_call(
        first_kernel,
        grid=(CAP,),
        in_specs=[smem(), smem(), smem(), smem(), whole(1, OWN, NODES), anywhere()],
        out_specs=[whole(NODES, BLK), whole(PACKED, BLK), whole(PACKED, BLK), cell_block, cell_block, anywhere()],
        out_shape=[struct(NODES, BLK), struct(PACKED, BLK), struct(PACKED, BLK), struct(CAP, CELL, CELL, dtype=BF16), struct(CAP, CELL, CELL, dtype=BF16), struct(NODES, BLK)],
        scratch_shapes=scratch(pltpu.VMEM((CAP, CELL, CELL), F32)),
        compiler_params=params(),
        name="first_step",
    )(live, nodes, upper, lower, start, ham)


def next_step(first, live, nodes, upper, lower, part, previous, above, below, high, low):
    cell_block = pl.BlockSpec((1, CELL, CELL), lambda c: (c, 0, 0))
    return pl.pallas_call(
        functools.partial(next_kernel, first),
        grid=(CAP,),
        in_specs=[smem(), smem(), smem(), smem(), whole(NODES, BLK), anywhere(), anywhere(), anywhere(), cell_block, cell_block],
        out_specs=[whole(NODES, BLK), whole(PACKED, BLK), whole(PACKED, BLK)] + [anywhere()] * first,
        out_shape=[struct(NODES, BLK), struct(PACKED, BLK), struct(PACKED, BLK)] + [struct(NODES, BLK)] * first,
        scratch_shapes=scratch(pltpu.VMEM((NODES, BLK), F32), pltpu.VMEM((2, PACKED, BLK), F32)),
        compiler_params=params(),
        name="second_step" if first else "third_step",
    )(live, nodes, upper, lower, part, previous, above, below, high, low)


def last_step(upper, lower, part, above, below):
    return pl.pallas_call(
        last_kernel,
        in_specs=[smem(), smem(), vmem(), vmem(), vmem()],
        out_specs=vmem(),
        out_shape=struct(4, OWN, COLS),
        scratch_shapes=[pltpu.VMEM((ROWS, BLK), F32), pltpu.VMEM((2, SHARE, BLK), F32)],
        compiler_params=params(),
        name="last_step",
    )(upper, lower, part, above, below)


def weight_step(lower):
    return pl.pallas_call(
        weight_kernel,
        in_specs=[smem()],
        out_specs=vmem(),
        out_shape=struct(8, NODES),
        scratch_shapes=[pltpu.VMEM((ROWS, BLK), F32)],
        compiler_params=params(),
        name="weight_step",
    )(lower)


def gram_step(quarter, own, weight):
    return pl.pallas_call(
        gram_kernel,
        grid_spec=pltpu.PrefetchScalarGridSpec(
            num_scalar_prefetch=1,
            grid=(1,),
            in_specs=[whole(COLS, COLS), pl.BlockSpec((8, COLS), lambda i, q: (0, q[0]))],
            out_specs=[whole(COLS, COLS), whole(6 * BLK, BLK)],
        ),
        out_shape=[struct(COLS, COLS), struct(6 * BLK, BLK)],
        compiler_params=params(),
        name="gram_step",
    )(quarter, own, weight)


def rotate_step(gram, rows):
    return pl.pallas_call(
        rotate_kernel,
        out_shape=struct(1, COLS, COLS),
        scratch_shapes=[pltpu.VMEM((BLK, 2 * BLK), F32), pltpu.VMEM((BLK, BLK), F32), pltpu.VMEM((48, BLK), BF16), pltpu.VMEM((48, 2 * BLK), BF16)],
        compiler_params=params(),
        name="rotate_step",
    )(gram, rows)


def exchange(up, low):
    last = 191
    from_above = lax.ppermute(low, SPACE, [(i + 1, i) for i in range(last)])
    from_below = lax.ppermute(up, SPACE, [(i, i + 1) for i in range(last)])
    return from_above, from_below


def scatter_sum(value, axes):
    parts = lax.axis_size(axes)
    pieces = lax.all_to_all(value.reshape(parts, -1, BLK), axes, 0, 0, tiled=True)
    return pieces.sum(0)


def total_sum(value, axes):
    parts = lax.axis_size(axes)
    copies = jnp.broadcast_to(value[None], (parts,) + value.shape)
    return lax.all_to_all(copies, axes, 0, 0, tiled=True).sum(0)


def spread(value, axes):
    parts = lax.axis_size(axes)
    copies = jnp.broadcast_to(value[None], (parts,) + value.shape)
    return lax.all_to_all(copies, axes, 0, 0, tiled=True).reshape(-1, BLK)


def shards(wavefunctions, cell_ham, cell_nodes, cell_count, upper_nodes, lower_nodes):
    nodes = cell_nodes.reshape(-1)
    upper = upper_nodes.reshape(-1)
    lower = lower_nodes.reshape(-1)
    start = jnp.swapaxes(wavefunctions, 1, 2)
    ham = jnp.swapaxes(cell_ham, 1, 2).reshape(CELL, CAP, CELL)
    part, up, low, ham_high, ham_low, previous = first_step(cell_count, nodes, upper, lower, start, ham)
    above, below = exchange(up, low)
    part, up, low, current = next_step(True, cell_count, nodes, upper, lower, part, previous, above, below, ham_high, ham_low)
    above, below = exchange(up, low)
    part, up, low = next_step(False, cell_count, nodes, upper, lower, part, current, above, below, ham_high, ham_low)
    above, below = exchange(up, low)
    filtered = last_step(upper, lower, part, above, below)
    own = lax.all_to_all(filtered, "orb", 0, 0, tiled=True).reshape(COLS, COLS)
    quarter = lax.axis_index("orb").astype(jnp.int32).reshape(1)
    rows, gram = gram_step(quarter, own, weight_step(lower))
    gram = spread(total_sum(scatter_sum(gram, NEAR), FAR), NEAR)
    return rotate_step(gram, rows)


def solution(mesh):
    fine = Mesh(mesh.devices.reshape(3, 8, 4, 2, 4), SPACE + ("orb",))
    in_specs = (
        P(SPACE, None, "orb"),
        P(SPACE, None, None, None),
        P(SPACE, None, None),
        P(SPACE),
        P(SPACE, None),
        P(SPACE, None),
    )
    out_specs = P(SPACE, "orb", None)
    return jax.shard_map(shards, mesh=fine, in_specs=in_specs, out_specs=out_specs, check_vma=False)
```

```python
import functools

import jax
import jax.numpy as jnp
from jax import lax
from jax.experimental import pallas as pl
from jax.experimental.pallas import tpu as pltpu
from jax.sharding import Mesh, PartitionSpec as P

DEGREE = 3
CAP = 4
CELL = 729
NODES = 1536
ROWS = 1544
COLS = 384
OWN = 96
SHARE = 512
BLK = 128

center_shift = 0.5
half_width = 2.0

SPACE = ("z_hi", "y", "x", "core")
NEAR = ("x", "core", "orb")
FAR = ("z_hi", "y")

F32 = jnp.float32
BF16 = jnp.bfloat16
NT = (((1,), (1,)), ((), ()))
NN = (((1,), (0,)), ((), ()))
TN = (((0,), (0,)), ((), ()))
VMEM_BYTES = 30 * 1024 * 1024


def halves(value):
    high = value.astype(BF16)
    low = (value - high.astype(F32)).astype(BF16)
    return high, low


def dot(a, b, dims):
    return lax.dot_general(a, b, dims, preferred_element_type=F32)


def dot_exact(a, b, dims):
    return lax.dot_general(a, b, dims, precision=lax.Precision.HIGHEST, preferred_element_type=F32)


def dot_three(a, b, dims):
    a_high, a_low = halves(a)
    b_high, b_low = halves(b)
    return dot(a_high, b_high, dims) + (dot(a_high, b_low, dims) + dot(a_low, b_high, dims))


def place_rims(arrived, upper_ref, lower_ref, above, below):
    step = 16
    arrived[...] = jnp.zeros_like(arrived)

    def some(i, carry):
        first = i * step
        up_rows = [above[pl.ds(first + j, 1), :] for j in range(step)]
        low_rows = [below[pl.ds(first + j, 1), :] for j in range(step)]
        for j in range(step):
            arrived[pl.ds(upper_ref[first + j], 1), :] = up_rows[j]
            arrived[pl.ds(lower_ref[first + j], 1), :] = low_rows[j]
        return carry

    lax.fori_loop(0, SHARE // step, some, 0)


def take_rims(field, upper_ref, lower_ref, up, low):
    step = 16

    def some(i, carry):
        first = i * step
        up_rows = [field[pl.ds(upper_ref[first + j], 1), :] for j in range(step)]
        low_rows = [field[pl.ds(lower_ref[first + j], 1), :] for j in range(step)]
        for j in range(step):
            up[pl.ds(first + j, 1), :] = up_rows[j]
            low[pl.ds(first + j, 1), :] = low_rows[j]
        return carry

    lax.fori_loop(0, SHARE // step, some, 0)


def pack_rims(rim, out):
    lane = lax.broadcasted_iota(jnp.int32, (BLK, BLK), 1)
    tail = rim[3 * BLK:, :]
    for j in range(3):
        moved = pltpu.roll(tail, OWN - 32 * j, 1)
        out[j * BLK:(j + 1) * BLK, :] = jnp.where(lane < OWN, rim[j * BLK:(j + 1) * BLK, :], moved)


def unpack_rims(packed, rim):
    lane = lax.broadcasted_iota(jnp.int32, (BLK, BLK), 1)
    rim[0:3 * BLK, :] = packed[...]
    tail = pltpu.roll(packed[0:BLK, :], 32, 1)
    tail = jnp.where(lane < 32, tail, pltpu.roll(packed[BLK:2 * BLK, :], 64, 1))
    rim[3 * BLK:, :] = jnp.where(lane < 64, tail, pltpu.roll(packed[2 * BLK:, :], 96, 1))


def take_cell(field, nodes_ref, cell, out):
    step = 27
    base = cell * CELL

    def some(i, carry):
        first = i * step
        rows = [field[pl.ds(nodes_ref[base + first + j], 1), :] for j in range(step)]
        for j in range(step):
            out[pl.ds(first + j, 1), :] = rows[j]
        return carry

    lax.fori_loop(0, CELL // step, some, 0)


def put_cell(parts, nodes_ref, slot, product):
    step = 27

    def some(i, carry):
        first = i * step
        rows = [product[pl.ds(first + j, 1), :] for j in range(step)]
        for j in range(step):
            parts[slot, pl.ds(nodes_ref[slot * CELL + first + j], 1), :] = rows[j]
        return carry

    lax.fori_loop(0, CELL // step, some, 0)


def put_cells(parts, nodes_ref, cell, live, product):
    for slot in range(CAP):
        @pl.when((cell == slot) & (slot < live))
        def _():
            put_cell(parts, nodes_ref, slot, product)


def multiply_cell(high, low, gathered, packed, product):
    rows_high, rows_low = halves(gathered[0:CELL, :])
    packed[:, 0:BLK] = rows_high
    packed[:, BLK:] = rows_low
    both = dot(high[...], packed[...], NN)
    rest = dot(low[...], packed[:, 0:BLK], NN)
    product[0:CELL, :] = both[:, 0:BLK] + (both[:, BLK:] + rest)


def finish_step(field, parts, total, rims, previous, scale, upper_ref, lower_ref, next_out, up_out, low_out):
    total[...] = (parts[0] + parts[1]) + (parts[2] + parts[3])
    take_rims(total, upper_ref, lower_ref, rims.at[0], rims.at[1])
    pack_rims(rims.at[0], up_out)
    pack_rims(rims.at[1], low_out)
    step = total[0:NODES, :] - center_shift * field[0:NODES, :]
    step = step * scale
    if previous is not None:
        step = step - previous[0:NODES, :]
    next_out[...] = step


def first_kernel(live_ref, nodes_ref, upper_ref, lower_ref, start_ref, ham_ref, next_out, up_out, low_out, high_out, low_part_out, field, parts, total, rims, gathered, packed, product, ham, sems):
    cell = pl.program_id(0)
    fetches = [pltpu.make_async_copy(ham_ref.at[:, slot, :], ham.at[slot], sems.at[slot]) for slot in range(CAP)]

    @pl.when(cell == 0)
    def _():
        for fetch in fetches:
            fetch.start()
        field[0:NODES, :] = jnp.concatenate([start_ref[0], jnp.zeros((BLK - OWN, NODES), F32)], axis=0).T
        field[NODES:, :] = jnp.zeros((ROWS - NODES, BLK), F32)
        parts[...] = jnp.zeros_like(parts)

    @pl.when(cell < live_ref[0])
    def _():
        take_cell(field, nodes_ref, cell, gathered)

    for slot in range(CAP):
        @pl.when(cell == slot)
        def _():
            fetches[slot].wait()

    @pl.when(cell < live_ref[0])
    def _():
        high, low = halves(ham[cell])
        high_out[cell] = high
        low_part_out[cell] = low

    @pl.when(cell < live_ref[0])
    def _():
        multiply_cell(high_out.at[cell], low_part_out.at[cell], gathered, packed, product)

    put_cells(parts, nodes_ref, cell, live_ref[0], product)

    @pl.when(cell == CAP - 1)
    def _():
        finish_step(field, parts, total, rims, None, 1.0 / half_width, upper_ref, lower_ref, next_out, up_out, low_out)


def next_kernel(first, live_ref, nodes_ref, upper_ref, lower_ref, part_ref, prev_ref, above_ref, below_ref, high_ref, low_ref, *rest):
    next_out, up_out, low_out, field, parts, total, rims, gathered, packed, product = rest
    cell = pl.program_id(0)

    @pl.when(cell == 0)
    def _():
        scale = 1.0 / half_width if first else 1.0
        parts[...] = jnp.zeros_like(parts)
        unpack_rims(above_ref, rims.at[0])
        unpack_rims(below_ref, rims.at[1])
        place_rims(total, upper_ref, lower_ref, rims.at[0], rims.at[1])
        field[0:NODES, :] = part_ref[...] + total[0:NODES, :] * scale
        field[NODES:, :] = jnp.zeros((ROWS - NODES, BLK), F32)

    @pl.when(cell < live_ref[0])
    def _():
        take_cell(field, nodes_ref, cell, gathered)
        multiply_cell(high_ref.at[cell], low_ref.at[cell], gathered, packed, product)

    put_cells(parts, nodes_ref, cell, live_ref[0], product)

    @pl.when(cell == CAP - 1)
    def _():
        finish_step(field, parts, total, rims, prev_ref, 1.0, upper_ref, lower_ref, next_out, up_out, low_out)


def last_kernel(upper_ref, lower_ref, part_ref, above_ref, below_ref, out, field, rims):
    unpack_rims(above_ref, rims.at[0])
    unpack_rims(below_ref, rims.at[1])
    place_rims(field, upper_ref, lower_ref, rims.at[0], rims.at[1])
    turned = (part_ref[...] + field[0:NODES, :]).T[0:OWN, :]
    for q in range(4):
        out[q] = turned[:, q * COLS:(q + 1) * COLS]


def weight_kernel(lower_ref, out, weight):
    weight[...] = jnp.full((ROWS, BLK), 1.0 / (192 * NODES), F32)
    nothing = jnp.zeros((1, BLK), F32)

    def some(i, carry):
        for j in range(16):
            weight[pl.ds(lower_ref[i * 16 + j], 1), :] = nothing
        return carry

    lax.fori_loop(0, SHARE // 16, some, 0)
    out[...] = weight[0:NODES, :].T[0:8, :]


def gram_kernel(quarter_ref, own_ref, weight_ref, rows_out, gram_out):
    del quarter_ref
    turned = own_ref[...]
    rows_out[...] = turned.T
    left_high, left_low = halves(turned * weight_ref[0:1, :])
    right_high, right_low = halves(turned)

    def block_row(k):
        a_high, a_low = left_high[k * BLK:(k + 1) * BLK], left_low[k * BLK:(k + 1) * BLK]
        b_high, b_low = right_high[:(k + 1) * BLK], right_low[:(k + 1) * BLK]
        return dot(a_high, b_high, NT) + (dot(a_high, b_low, NT) + dot(a_low, b_high, NT))

    first, second, third = block_row(0), block_row(1), block_row(2)
    blocks = [first, second[:, :BLK], third[:, :BLK], second[:, BLK:], third[:, BLK:2 * BLK], third[:, 2 * BLK:]]
    for k, block in enumerate(blocks):
        gram_out[k * BLK:(k + 1) * BLK, :] = block


def inverse_factor(work, inverse, left_ref, right_ref):
    sub = lax.broadcasted_iota(jnp.int32, (8, BLK), 0)
    lane = lax.broadcasted_iota(jnp.int32, (8, BLK), 1)
    left_ref[...] = jnp.zeros_like(left_ref)
    right_ref[...] = jnp.zeros_like(right_ref)

    def three(v):
        v1 = v.astype(BF16).astype(F32)
        rest = v - v1
        v2 = rest.astype(BF16).astype(F32)
        return v1, v2, rest - v2

    def panel(p, carry):
        panel_a, panel_i = carry
        first = pl.multiple_of(p * 8, 8)
        work[...] = work[...] - dot(left_ref[...], right_ref[...], TN)
        columns = [jnp.broadcast_to(jnp.sum(jnp.where(lane == first + k, panel_a, 0.0), axis=1, keepdims=True), (8, BLK)) for k in range(8)]
        e = {(i, k): jnp.broadcast_to(columns[k][i:i + 1, :], (8, BLK)) for i in range(8) for k in range(i + 1)}
        rows_a = [jnp.broadcast_to(panel_a[i:i + 1, :], (8, BLK)) for i in range(8)]
        rows_i = [jnp.broadcast_to(panel_i[i:i + 1, :], (8, BLK)) for i in range(8)]
        for k in range(8):
            pivot = e[k, k]
            r = lax.rsqrt(pivot)
            rows_a[k] = rows_a[k] * r
            rows_i[k] = rows_i[k] * r
            below = {i: e[i, k] * r for i in range(k + 1, 8)}
            for i in range(k + 1, 8):
                for j in range(k + 1, i + 1):
                    e[i, j] = e[i, j] - below[i] * below[j]
                rows_a[i] = rows_a[i] - below[i] * rows_a[k]
                rows_i[i] = rows_i[i] - below[i] * rows_i[k]
        new_a, new_i = rows_a[0], rows_i[0]
        for k in range(1, 8):
            new_a = jnp.where(sub == k, rows_a[k], new_a)
            new_i = jnp.where(sub == k, rows_i[k], new_i)
        inverse[pl.ds(first, 8), :] = new_i
        a1, a2, a3 = three(new_a)
        b1, b2, b3 = three(jnp.concatenate([new_a, new_i], axis=1))
        left_ref[...] = jnp.concatenate([a1, a1, a2, a1, a2, a3], axis=0).astype(BF16)
        right_ref[...] = jnp.concatenate([b1, b2, b1, b3, b2, b1], axis=0).astype(BF16)
        following = pl.multiple_of(jnp.minimum(first + 8, BLK - 8), 8)
        next_a = work[pl.ds(following, 8), 0:BLK]
        next_i = work[pl.ds(following, 8), BLK:]
        for k in range(8):
            factor = jnp.sum(jnp.where(lane == sub + (first + 8), rows_a[k], 0.0), axis=1, keepdims=True)
            next_a = next_a - factor * rows_a[k]
            next_i = next_i - factor * rows_i[k]
        return next_a, next_i

    lax.fori_loop(0, BLK // 8, panel, (work[0:8, 0:BLK], work[0:8, BLK:]))


def rotate_kernel(gram_ref, rows_ref, out, work, inverse, left_ref, right_ref):
    eye = (lax.broadcasted_iota(jnp.int32, (BLK, BLK), 0) == lax.broadcasted_iota(jnp.int32, (BLK, BLK), 1)).astype(F32)

    def factor(block):
        work[:, 0:BLK] = block
        work[:, BLK:] = eye
        inverse_factor(work, inverse, left_ref, right_ref)
        return inverse[...]

    m1 = factor(gram_ref[0:BLK, :])
    left = dot_exact(gram_ref[BLK:3 * BLK, :], m1, NT)
    l21, l31 = left[0:BLK], left[BLK:]
    m2 = factor(gram_ref[3 * BLK:4 * BLK, :] - dot_exact(l21, l21, NT))
    l32 = dot_exact(gram_ref[4 * BLK:5 * BLK, :] - dot_exact(l31, l21, NT), m2, NT)
    rows = rows_ref[...]
    z1 = dot_three(rows[:, 0:BLK], m1, NT)
    out[0, :, 0:BLK] = z1
    z2 = dot_three(rows[:, BLK:2 * BLK] - dot_three(z1, l21, NT), m2, NT)
    out[0, :, BLK:2 * BLK] = z2
    m3 = factor(gram_ref[5 * BLK:, :] - dot_exact(l31, l31, NT) - dot_exact(l32, l32, NT))
    z3 = dot_three(rows[:, 2 * BLK:] - dot_three(z1, l31, NT) - dot_three(z2, l32, NT), m3, NT)
    out[0, :, 2 * BLK:] = z3


def smem():
    return pl.BlockSpec(memory_space=pltpu.SMEM)


def vmem():
    return pl.BlockSpec(memory_space=pltpu.VMEM)


def whole(*shape):
    return pl.BlockSpec(shape, lambda *_: (0,) * len(shape))


def params():
    return pltpu.CompilerParams(vmem_limit_bytes=VMEM_BYTES)


def scratch(*more):
    return [
        *more,
        pltpu.VMEM((CAP, ROWS, BLK), F32),
        pltpu.VMEM((ROWS, BLK), F32),
        pltpu.VMEM((2, SHARE, BLK), F32),
        pltpu.VMEM((736, BLK), F32),
        pltpu.VMEM((CELL, 2 * BLK), BF16),
        pltpu.VMEM((736, BLK), F32),
    ]


def struct(*shape, dtype=F32):
    return jax.ShapeDtypeStruct(shape, dtype)


PACKED = 3 * BLK


def first_step(live, nodes, upper, lower, start, ham):
    return pl.pallas_call(
        first_kernel,
        grid=(CAP,),
        in_specs=[smem(), smem(), smem(), smem(), whole(1, OWN, NODES), pl.BlockSpec(memory_space=pltpu.HBM)],
        out_specs=[vmem(), whole(PACKED, BLK), whole(PACKED, BLK), vmem(), vmem(), vmem()],
        out_shape=[pltpu.VMEM((NODES, BLK), F32), struct(PACKED, BLK), struct(PACKED, BLK), pltpu.VMEM((CAP, CELL, CELL), BF16), pltpu.VMEM((CAP, CELL, CELL), BF16), pltpu.VMEM((ROWS, BLK), F32)],
        scratch_shapes=scratch() + [pltpu.VMEM((CAP, CELL, CELL), F32), pltpu.SemaphoreType.DMA((CAP,))],
        compiler_params=params(),
        name="first_step",
    )(live, nodes, upper, lower, start, ham)


def next_step(first, live, nodes, upper, lower, part, previous, above, below, high, low):
    field_out = pltpu.VMEM((ROWS, BLK), F32)
    return pl.pallas_call(
        functools.partial(next_kernel, first),
        grid=(CAP,),
        in_specs=[smem(), smem(), smem(), smem()] + [vmem()] * 6,
        out_specs=[vmem(), whole(PACKED, BLK), whole(PACKED, BLK)] + [vmem()] * first,
        out_shape=[pltpu.VMEM((NODES, BLK), F32), struct(PACKED, BLK), struct(PACKED, BLK)] + [field_out] * first,
        scratch_shapes=scratch(*[field_out] * (not first)),
        compiler_params=params(),
        name="second_step" if first else "third_step",
    )(live, nodes, upper, lower, part, previous, above, below, high, low)


def last_step(upper, lower, part, above, below):
    return pl.pallas_call(
        last_kernel,
        in_specs=[smem(), smem(), vmem(), vmem(), vmem()],
        out_specs=vmem(),
        out_shape=struct(4, OWN, COLS),
        scratch_shapes=[pltpu.VMEM((ROWS, BLK), F32), pltpu.VMEM((2, SHARE, BLK), F32)],
        compiler_params=params(),
        name="last_step",
    )(upper, lower, part, above, below)


def weight_step(lower):
    return pl.pallas_call(
        weight_kernel,
        in_specs=[smem()],
        out_specs=vmem(),
        out_shape=struct(8, NODES),
        scratch_shapes=[pltpu.VMEM((ROWS, BLK), F32)],
        compiler_params=params(),
        name="weight_step",
    )(lower)


def gram_step(quarter, own, weight):
    return pl.pallas_call(
        gram_kernel,
        grid_spec=pltpu.PrefetchScalarGridSpec(
            num_scalar_prefetch=1,
            grid=(1,),
            in_specs=[vmem(), pl.BlockSpec((8, COLS), lambda i, q: (0, q[0]))],
            out_specs=[vmem(), whole(6 * BLK, BLK)],
        ),
        out_shape=[pltpu.VMEM((COLS, COLS), F32), struct(6 * BLK, BLK)],
        compiler_params=params(),
        name="gram_step",
    )(quarter, own, weight)


def rotate_step(gram, rows):
    return pl.pallas_call(
        rotate_kernel,
        in_specs=[vmem(), vmem()],
        out_specs=vmem(),
        out_shape=struct(1, COLS, COLS),
        scratch_shapes=[pltpu.VMEM((BLK, 2 * BLK), F32), pltpu.VMEM((BLK, BLK), F32), pltpu.VMEM((48, BLK), BF16), pltpu.VMEM((48, 2 * BLK), BF16)],
        compiler_params=params(),
        name="rotate_step",
    )(gram, rows)


def near_core(value):
    return pltpu.with_memory_space_constraint(value, pltpu.VMEM)


def exchange(up, low):
    last = 191
    from_above = lax.ppermute(low, SPACE, [(i + 1, i) for i in range(last)])
    from_below = lax.ppermute(up, SPACE, [(i, i + 1) for i in range(last)])
    return near_core(from_above), near_core(from_below)


def scatter_sum(value, axes):
    parts = lax.axis_size(axes)
    pieces = lax.all_to_all(value.reshape(parts, -1, BLK), axes, 0, 0, tiled=True)
    return pieces.sum(0)


def total_sum(value, axes):
    parts = lax.axis_size(axes)
    copies = jnp.broadcast_to(value[None], (parts,) + value.shape)
    return lax.all_to_all(copies, axes, 0, 0, tiled=True).sum(0)


def spread(value, axes):
    parts = lax.axis_size(axes)
    copies = jnp.broadcast_to(value[None], (parts,) + value.shape)
    return lax.all_to_all(copies, axes, 0, 0, tiled=True).reshape(-1, BLK)


def shards(wavefunctions, cell_ham, cell_nodes, cell_count, upper_nodes, lower_nodes):
    nodes = cell_nodes.reshape(-1)
    upper = upper_nodes.reshape(-1)
    lower = lower_nodes.reshape(-1)
    start = jnp.swapaxes(wavefunctions, 1, 2)
    ham = jnp.swapaxes(cell_ham, 1, 2).reshape(CELL, CAP, CELL)
    ham = pltpu.with_memory_space_constraint(ham, pltpu.HBM)
    part, up, low, ham_high, ham_low, previous = first_step(cell_count, nodes, upper, lower, start, ham)
    above, below = exchange(up, low)
    part, up, low, current = next_step(True, cell_count, nodes, upper, lower, part, previous, above, below, ham_high, ham_low)
    above, below = exchange(up, low)
    part, up, low = next_step(False, cell_count, nodes, upper, lower, part, current, above, below, ham_high, ham_low)
    above, below = exchange(up, low)
    filtered = last_step(upper, lower, part, above, below)
    own = near_core(lax.all_to_all(filtered, "orb", 0, 0, tiled=True).reshape(COLS, COLS))
    quarter = lax.axis_index("orb").astype(jnp.int32).reshape(1)
    rows, gram = gram_step(quarter, own, weight_step(lower))
    gram = spread(total_sum(scatter_sum(gram, NEAR), FAR), NEAR)
    return rotate_step(near_core(gram), rows)


def solution(mesh):
    fine = Mesh(mesh.devices.reshape(3, 8, 4, 2, 4), SPACE + ("orb",))
    in_specs = (
        P(SPACE, None, "orb"),
        P(SPACE, None, None, None),
        P(SPACE, None, None),
        P(SPACE),
        P(SPACE, None),
        P(SPACE, None),
    )
    out_specs = P(SPACE, "orb", None)
    return jax.shard_map(shards, mesh=fine, in_specs=in_specs, out_specs=out_specs, check_vma=False)
```

```python
import functools

import jax
import jax.numpy as jnp
from jax import lax
from jax.experimental import pallas as pl
from jax.experimental.pallas import tpu as pltpu
from jax.sharding import Mesh, PartitionSpec as P

DEGREE = 3
CAP = 4
CELL = 729
NODES = 1536
ROWS = 1544
COLS = 384
OWN = 96
SHARE = 512
BLK = 128

center_shift = 0.5
half_width = 2.0

SPACE = ("z_hi", "y", "x", "core")
NEAR = ("x", "core", "orb")
FAR = ("z_hi", "y")

F32 = jnp.float32
BF16 = jnp.bfloat16
NT = (((1,), (1,)), ((), ()))
NN = (((1,), (0,)), ((), ()))
TN = (((0,), (0,)), ((), ()))
VMEM_BYTES = 30 * 1024 * 1024


def halves(value):
    high = value.astype(BF16)
    low = (value - high.astype(F32)).astype(BF16)
    return high, low


def dot(a, b, dims):
    return lax.dot_general(a, b, dims, preferred_element_type=F32)


def dot_exact(a, b, dims):
    return lax.dot_general(a, b, dims, precision=lax.Precision.HIGHEST, preferred_element_type=F32)


def dot_three(a, b, dims):
    a_high, a_low = halves(a)
    b_high, b_low = halves(b)
    return dot(a_high, b_high, dims) + (dot(a_high, b_low, dims) + dot(a_low, b_high, dims))


class Part:
    def __init__(self, lists, first):
        self.lists, self.first = lists, first

    def __getitem__(self, index):
        return self.lists[self.first + index]


def split_lists(lists):
    return Part(lists, 0), Part(lists, CAP * CELL), Part(lists, CAP * CELL + SHARE)


def place_rims(arrived, upper_ref, lower_ref, above, below):
    step = 16
    arrived[...] = jnp.zeros_like(arrived)

    def some(i, carry):
        first = i * step
        up_rows = [above[pl.ds(first + j, 1), :] for j in range(step)]
        low_rows = [below[pl.ds(first + j, 1), :] for j in range(step)]
        for j in range(step):
            arrived[pl.ds(upper_ref[first + j], 1), :] = up_rows[j]
            arrived[pl.ds(lower_ref[first + j], 1), :] = low_rows[j]
        return carry

    lax.fori_loop(0, SHARE // step, some, 0)


def take_rims(field, upper_ref, lower_ref, up, low):
    step = 16

    def some(i, carry):
        first = i * step
        up_rows = [field[pl.ds(upper_ref[first + j], 1), :] for j in range(step)]
        low_rows = [field[pl.ds(lower_ref[first + j], 1), :] for j in range(step)]
        for j in range(step):
            up[pl.ds(first + j, 1), :] = up_rows[j]
            low[pl.ds(first + j, 1), :] = low_rows[j]
        return carry

    lax.fori_loop(0, SHARE // step, some, 0)


def pack_rims(rim, out):
    lane = lax.broadcasted_iota(jnp.int32, (BLK, BLK), 1)
    tail = rim[3 * BLK:, :]
    for j in range(3):
        moved = pltpu.roll(tail, OWN - 32 * j, 1)
        out[j * BLK:(j + 1) * BLK, :] = jnp.where(lane < OWN, rim[j * BLK:(j + 1) * BLK, :], moved)


def unpack_rims(packed, rim):
    lane = lax.broadcasted_iota(jnp.int32, (BLK, BLK), 1)
    rim[0:3 * BLK, :] = packed[...]
    tail = pltpu.roll(packed[0:BLK, :], 32, 1)
    tail = jnp.where(lane < 32, tail, pltpu.roll(packed[BLK:2 * BLK, :], 64, 1))
    rim[3 * BLK:, :] = jnp.where(lane < 64, tail, pltpu.roll(packed[2 * BLK:, :], 96, 1))


def take_cell(field, nodes_ref, cell, out):
    step = 27
    base = cell * CELL

    def some(i, carry):
        first = i * step
        rows = [field[pl.ds(nodes_ref[base + first + j], 1), :] for j in range(step)]
        for j in range(step):
            out[pl.ds(first + j, 1), :] = rows[j]
        return carry

    lax.fori_loop(0, CELL // step, some, 0)


def put_cell(parts, nodes_ref, slot, product):
    step = 27

    def some(i, carry):
        first = i * step
        rows = [product[pl.ds(first + j, 1), :] for j in range(step)]
        for j in range(step):
            parts[slot, pl.ds(nodes_ref[slot * CELL + first + j], 1), :] = rows[j]
        return carry

    lax.fori_loop(0, CELL // step, some, 0)


def put_cells(parts, nodes_ref, cell, live, product):
    for slot in range(CAP):
        @pl.when((cell == slot) & (slot < live))
        def _():
            put_cell(parts, nodes_ref, slot, product)


def multiply_cell(high, low, gathered, packed, product):
    rows_high, rows_low = halves(gathered[0:CELL, :])
    packed[:, 0:BLK] = rows_high
    packed[:, BLK:] = rows_low
    both = dot(high[...], packed[...], NN)
    rest = dot(low[...], packed[:, 0:BLK], NN)
    product[0:CELL, :] = both[:, 0:BLK] + (both[:, BLK:] + rest)


def finish_step(field, parts, total, rims, previous, scale, upper_ref, lower_ref, next_out, up_out, low_out):
    total[...] = (parts[0] + parts[1]) + (parts[2] + parts[3])
    take_rims(total, upper_ref, lower_ref, rims.at[0], rims.at[1])
    pack_rims(rims.at[0], up_out)
    pack_rims(rims.at[1], low_out)
    step = total[0:NODES, :] - center_shift * field[0:NODES, :]
    step = step * scale
    if previous is not None:
        step = step - previous[0:NODES, :]
    next_out[...] = step


def first_kernel(live_ref, lists_ref, start_ref, ham_ref, next_out, up_out, low_out, high_out, low_part_out, field, parts, total, rims, gathered, packed, product, ham, begin, sems):
    nodes_ref, upper_ref, lower_ref = split_lists(lists_ref)
    cell = pl.program_id(0)
    fetches = [pltpu.make_async_copy(ham_ref.at[:, slot, :], ham.at[slot], sems.at[slot]) for slot in range(CAP)]

    @pl.when(cell == 0)
    def _():
        first_fetch = pltpu.make_async_copy(start_ref, begin, sems.at[CAP])
        first_fetch.start()
        for fetch in fetches:
            fetch.start()
        parts[...] = jnp.zeros_like(parts)
        first_fetch.wait()
        field[0:NODES, :] = jnp.concatenate([begin[0], jnp.zeros((BLK - OWN, NODES), F32)], axis=0).T
        field[NODES:, :] = jnp.zeros((ROWS - NODES, BLK), F32)

    @pl.when(cell < live_ref[0])
    def _():
        take_cell(field, nodes_ref, cell, gathered)

    for slot in range(CAP):
        @pl.when(cell == slot)
        def _():
            fetches[slot].wait()

    @pl.when(cell < live_ref[0])
    def _():
        high, low = halves(ham[cell])
        high_out[cell] = high
        low_part_out[cell] = low

    @pl.when(cell < live_ref[0])
    def _():
        multiply_cell(high_out.at[cell], low_part_out.at[cell], gathered, packed, product)

    put_cells(parts, nodes_ref, cell, live_ref[0], product)

    @pl.when(cell == CAP - 1)
    def _():
        finish_step(field, parts, total, rims, None, 1.0 / half_width, upper_ref, lower_ref, next_out, up_out, low_out)


def next_kernel(first, live_ref, lists_ref, part_ref, prev_ref, above_ref, below_ref, high_ref, low_ref, *rest):
    next_out, up_out, low_out, field, parts, total, rims, gathered, packed, product = rest
    nodes_ref, upper_ref, lower_ref = split_lists(lists_ref)
    cell = pl.program_id(0)

    @pl.when(cell == 0)
    def _():
        scale = 1.0 / half_width if first else 1.0
        parts[...] = jnp.zeros_like(parts)
        unpack_rims(above_ref, rims.at[0])
        unpack_rims(below_ref, rims.at[1])
        place_rims(total, upper_ref, lower_ref, rims.at[0], rims.at[1])
        field[0:NODES, :] = part_ref[...] + total[0:NODES, :] * scale
        field[NODES:, :] = jnp.zeros((ROWS - NODES, BLK), F32)

    @pl.when(cell < live_ref[0])
    def _():
        take_cell(field, nodes_ref, cell, gathered)
        multiply_cell(high_ref.at[cell], low_ref.at[cell], gathered, packed, product)

    put_cells(parts, nodes_ref, cell, live_ref[0], product)

    @pl.when(cell == CAP - 1)
    def _():
        finish_step(field, parts, total, rims, prev_ref, 1.0, upper_ref, lower_ref, next_out, up_out, low_out)


def last_kernel(lists_ref, part_ref, above_ref, below_ref, out, field, rims):
    _, upper_ref, lower_ref = split_lists(lists_ref)
    unpack_rims(above_ref, rims.at[0])
    unpack_rims(below_ref, rims.at[1])
    place_rims(field, upper_ref, lower_ref, rims.at[0], rims.at[1])
    turned = (part_ref[...] + field[0:NODES, :]).T[0:OWN, :]
    for q in range(4):
        out[q] = turned[:, q * COLS:(q + 1) * COLS]


def weight_kernel(lists_ref, out, weight):
    lower_ref = split_lists(lists_ref)[2]
    weight[...] = jnp.full((ROWS, BLK), 1.0 / (192 * NODES), F32)
    nothing = jnp.zeros((1, BLK), F32)

    def some(i, carry):
        for j in range(16):
            weight[pl.ds(lower_ref[i * 16 + j], 1), :] = nothing
        return carry

    lax.fori_loop(0, SHARE // 16, some, 0)
    out[...] = weight[0:NODES, :].T[0:8, :]


def gram_kernel(quarter_ref, own_ref, weight_ref, rows_out, gram_out):
    del quarter_ref
    turned = own_ref[...]
    rows_out[...] = turned.T
    left_high, left_low = halves(turned * weight_ref[0:1, :])
    right_high, right_low = halves(turned)

    def block_row(k):
        a_high, a_low = left_high[k * BLK:(k + 1) * BLK], left_low[k * BLK:(k + 1) * BLK]
        b_high, b_low = right_high[:(k + 1) * BLK], right_low[:(k + 1) * BLK]
        return dot(a_high, b_high, NT) + (dot(a_high, b_low, NT) + dot(a_low, b_high, NT))

    first, second, third = block_row(0), block_row(1), block_row(2)
    blocks = [first, second[:, :BLK], third[:, :BLK], second[:, BLK:], third[:, BLK:2 * BLK], third[:, 2 * BLK:]]
    for k, block in enumerate(blocks):
        gram_out[k * BLK:(k + 1) * BLK, :] = block


def inverse_factor(work, inverse, left_ref, right_ref):
    sub = lax.broadcasted_iota(jnp.int32, (8, BLK), 0)
    lane = lax.broadcasted_iota(jnp.int32, (8, BLK), 1)
    left_ref[...] = jnp.zeros_like(left_ref)
    right_ref[...] = jnp.zeros_like(right_ref)

    def three(v):
        v1 = v.astype(BF16).astype(F32)
        rest = v - v1
        v2 = rest.astype(BF16).astype(F32)
        return v1, v2, rest - v2

    def panel(p, carry):
        panel_a, panel_i = carry
        first = pl.multiple_of(p * 8, 8)
        work[...] = work[...] - dot(left_ref[...], right_ref[...], TN)
        columns = [jnp.broadcast_to(jnp.sum(jnp.where(lane == first + k, panel_a, 0.0), axis=1, keepdims=True), (8, BLK)) for k in range(8)]
        e = {(i, k): jnp.broadcast_to(columns[k][i:i + 1, :], (8, BLK)) for i in range(8) for k in range(i + 1)}
        rows_a = [jnp.broadcast_to(panel_a[i:i + 1, :], (8, BLK)) for i in range(8)]
        rows_i = [jnp.broadcast_to(panel_i[i:i + 1, :], (8, BLK)) for i in range(8)]
        for k in range(8):
            pivot = e[k, k]
            r = lax.rsqrt(pivot)
            rows_a[k] = rows_a[k] * r
            rows_i[k] = rows_i[k] * r
            below = {i: e[i, k] * r for i in range(k + 1, 8)}
            for i in range(k + 1, 8):
                for j in range(k + 1, i + 1):
                    e[i, j] = e[i, j] - below[i] * below[j]
                rows_a[i] = rows_a[i] - below[i] * rows_a[k]
                rows_i[i] = rows_i[i] - below[i] * rows_i[k]
        new_a, new_i = rows_a[0], rows_i[0]
        for k in range(1, 8):
            new_a = jnp.where(sub == k, rows_a[k], new_a)
            new_i = jnp.where(sub == k, rows_i[k], new_i)
        inverse[pl.ds(first, 8), :] = new_i
        a1, a2, a3 = three(new_a)
        b1, b2, b3 = three(jnp.concatenate([new_a, new_i], axis=1))
        left_ref[...] = jnp.concatenate([a1, a1, a2, a1, a2, a3], axis=0).astype(BF16)
        right_ref[...] = jnp.concatenate([b1, b2, b1, b3, b2, b1], axis=0).astype(BF16)
        following = pl.multiple_of(jnp.minimum(first + 8, BLK - 8), 8)
        next_a = work[pl.ds(following, 8), 0:BLK]
        next_i = work[pl.ds(following, 8), BLK:]
        for k in range(8):
            factor = jnp.sum(jnp.where(lane == sub + (first + 8), rows_a[k], 0.0), axis=1, keepdims=True)
            next_a = next_a - factor * rows_a[k]
            next_i = next_i - factor * rows_i[k]
        return next_a, next_i

    lax.fori_loop(0, BLK // 8, panel, (work[0:8, 0:BLK], work[0:8, BLK:]))


def rotate_kernel(gram_ref, rows_ref, out, work, inverse, left_ref, right_ref):
    eye = (lax.broadcasted_iota(jnp.int32, (BLK, BLK), 0) == lax.broadcasted_iota(jnp.int32, (BLK, BLK), 1)).astype(F32)

    def factor(block):
        work[:, 0:BLK] = block
        work[:, BLK:] = eye
        inverse_factor(work, inverse, left_ref, right_ref)
        return inverse[...]

    m1 = factor(gram_ref[0:BLK, :])
    left = dot_exact(gram_ref[BLK:3 * BLK, :], m1, NT)
    l21, l31 = left[0:BLK], left[BLK:]
    m2 = factor(gram_ref[3 * BLK:4 * BLK, :] - dot_exact(l21, l21, NT))
    l32 = dot_exact(gram_ref[4 * BLK:5 * BLK, :] - dot_exact(l31, l21, NT), m2, NT)
    rows = rows_ref[...]
    z1 = dot_three(rows[:, 0:BLK], m1, NT)
    out[0, :, 0:BLK] = z1
    z2 = dot_three(rows[:, BLK:2 * BLK] - dot_three(z1, l21, NT), m2, NT)
    out[0, :, BLK:2 * BLK] = z2
    m3 = factor(gram_ref[5 * BLK:, :] - dot_exact(l31, l31, NT) - dot_exact(l32, l32, NT))
    z3 = dot_three(rows[:, 2 * BLK:] - dot_three(z1, l31, NT) - dot_three(z2, l32, NT), m3, NT)
    out[0, :, 2 * BLK:] = z3


def smem():
    return pl.BlockSpec(memory_space=pltpu.SMEM)


def hbm():
    return pl.BlockSpec(memory_space=pltpu.HBM)


def vmem():
    return pl.BlockSpec(memory_space=pltpu.VMEM)


def whole(*shape):
    return pl.BlockSpec(shape, lambda *_: (0,) * len(shape))


def params():
    return pltpu.CompilerParams(vmem_limit_bytes=VMEM_BYTES)


def scratch(*more):
    return [
        *more,
        pltpu.VMEM((CAP, ROWS, BLK), F32),
        pltpu.VMEM((ROWS, BLK), F32),
        pltpu.VMEM((2, SHARE, BLK), F32),
        pltpu.VMEM((736, BLK), F32),
        pltpu.VMEM((CELL, 2 * BLK), BF16),
        pltpu.VMEM((736, BLK), F32),
    ]


def struct(*shape, dtype=F32):
    return jax.ShapeDtypeStruct(shape, dtype)


PACKED = 3 * BLK


def first_step(live, lists, start, ham):
    return pl.pallas_call(
        first_kernel,
        grid=(CAP,),
        in_specs=[smem(), smem(), hbm(), hbm()],
        out_specs=[vmem(), whole(PACKED, BLK), whole(PACKED, BLK), vmem(), vmem(), vmem()],
        out_shape=[pltpu.VMEM((NODES, BLK), F32), struct(PACKED, BLK), struct(PACKED, BLK), pltpu.VMEM((CAP, CELL, CELL), BF16), pltpu.VMEM((CAP, CELL, CELL), BF16), pltpu.VMEM((ROWS, BLK), F32)],
        scratch_shapes=scratch() + [pltpu.VMEM((CAP, CELL, CELL), F32), pltpu.VMEM((1, OWN, NODES), F32), pltpu.SemaphoreType.DMA((CAP + 1,))],
        compiler_params=params(),
        name="first_step",
    )(live, lists, start, ham)


def next_step(first, live, lists, part, previous, above, below, high, low):
    field_out = pltpu.VMEM((ROWS, BLK), F32)
    return pl.pallas_call(
        functools.partial(next_kernel, first),
        grid=(CAP,),
        in_specs=[smem(), smem()] + [vmem()] * 6,
        out_specs=[vmem(), whole(PACKED, BLK), whole(PACKED, BLK)] + [vmem()] * first,
        out_shape=[pltpu.VMEM((NODES, BLK), F32), struct(PACKED, BLK), struct(PACKED, BLK)] + [field_out] * first,
        scratch_shapes=scratch(*[field_out] * (not first)),
        compiler_params=params(),
        name="second_step" if first else "third_step",
    )(live, lists, part, previous, above, below, high, low)


def last_step(lists, part, above, below):
    return pl.pallas_call(
        last_kernel,
        in_specs=[smem(), vmem(), vmem(), vmem()],
        out_specs=vmem(),
        out_shape=struct(4, OWN, COLS),
        scratch_shapes=[pltpu.VMEM((ROWS, BLK), F32), pltpu.VMEM((2, SHARE, BLK), F32)],
        compiler_params=params(),
        name="last_step",
    )(lists, part, above, below)


def weight_step(lists):
    return pl.pallas_call(
        weight_kernel,
        in_specs=[smem()],
        out_specs=vmem(),
        out_shape=struct(8, NODES),
        scratch_shapes=[pltpu.VMEM((ROWS, BLK), F32)],
        compiler_params=params(),
        name="weight_step",
    )(lists)


def gram_step(quarter, own, weight):
    return pl.pallas_call(
        gram_kernel,
        grid_spec=pltpu.PrefetchScalarGridSpec(
            num_scalar_prefetch=1,
            grid=(1,),
            in_specs=[vmem(), pl.BlockSpec((8, COLS), lambda i, q: (0, q[0]))],
            out_specs=[vmem(), whole(6 * BLK, BLK)],
        ),
        out_shape=[pltpu.VMEM((COLS, COLS), F32), struct(6 * BLK, BLK)],
        compiler_params=params(),
        name="gram_step",
    )(quarter, own, weight)


def rotate_step(gram, rows):
    return pl.pallas_call(
        rotate_kernel,
        in_specs=[vmem(), vmem()],
        out_specs=vmem(),
        out_shape=struct(1, COLS, COLS),
        scratch_shapes=[pltpu.VMEM((BLK, 2 * BLK), F32), pltpu.VMEM((BLK, BLK), F32), pltpu.VMEM((48, BLK), BF16), pltpu.VMEM((48, 2 * BLK), BF16)],
        compiler_params=params(),
        name="rotate_step",
    )(gram, rows)


def near_core(value):
    return pltpu.with_memory_space_constraint(value, pltpu.VMEM)


def exchange(up, low):
    last = 191
    from_above = lax.ppermute(low, SPACE, [(i + 1, i) for i in range(last)])
    from_below = lax.ppermute(up, SPACE, [(i, i + 1) for i in range(last)])
    return near_core(from_above), near_core(from_below)


def scatter_sum(value, axes):
    parts = lax.axis_size(axes)
    pieces = lax.all_to_all(value.reshape(parts, -1, BLK), axes, 0, 0, tiled=True)
    return pieces.sum(0)


def total_sum(value, axes):
    parts = lax.axis_size(axes)
    copies = jnp.broadcast_to(value[None], (parts,) + value.shape)
    return lax.all_to_all(copies, axes, 0, 0, tiled=True).sum(0)


def spread(value, axes):
    parts = lax.axis_size(axes)
    copies = jnp.broadcast_to(value[None], (parts,) + value.shape)
    return lax.all_to_all(copies, axes, 0, 0, tiled=True).reshape(-1, BLK)


def shards(wavefunctions, cell_ham, cell_nodes, cell_count, upper_nodes, lower_nodes):
    lists = jnp.concatenate([cell_nodes.reshape(-1), upper_nodes.reshape(-1), lower_nodes.reshape(-1)])
    start = pltpu.with_memory_space_constraint(jnp.swapaxes(wavefunctions, 1, 2), pltpu.HBM)
    ham = jnp.swapaxes(cell_ham, 1, 2).reshape(CELL, CAP, CELL)
    ham = pltpu.with_memory_space_constraint(ham, pltpu.HBM)
    part, up, low, ham_high, ham_low, previous = first_step(cell_count, lists, start, ham)
    above, below = exchange(up, low)
    part, up, low, current = next_step(True, cell_count, lists, part, previous, above, below, ham_high, ham_low)
    above, below = exchange(up, low)
    part, up, low = next_step(False, cell_count, lists, part, current, above, below, ham_high, ham_low)
    above, below = exchange(up, low)
    filtered = last_step(lists, part, above, below)
    own = near_core(lax.all_to_all(filtered, "orb", 0, 0, tiled=True).reshape(COLS, COLS))
    quarter = lax.axis_index("orb").astype(jnp.int32).reshape(1)
    rows, gram = gram_step(quarter, own, weight_step(lists))
    gram = spread(total_sum(scatter_sum(gram, NEAR), FAR), NEAR)
    return rotate_step(near_core(gram), rows)


def solution(mesh):
    fine = Mesh(mesh.devices.reshape(3, 8, 4, 2, 4), SPACE + ("orb",))
    in_specs = (
        P(SPACE, None, "orb"),
        P(SPACE, None, None, None),
        P(SPACE, None, None),
        P(SPACE),
        P(SPACE, None),
        P(SPACE, None),
    )
    out_specs = P(SPACE, "orb", None)
    return jax.shard_map(shards, mesh=fine, in_specs=in_specs, out_specs=out_specs, check_vma=False)
```
